32 devices in a mesh: tok: 8 (over z, y), exp: 4 (over x, core).
Axes of the slice: x: 2, y: 2, z: 4, core: 2. Of those that a mesh axis runs over, the one named last changes fastest.
Arguments:
- tokens: bfloat16 [12, 8192, 1024], P(None, 'tok'), may hold values from -24 to 24
- slot_params: bfloat16 [1024, 128], P(None, 'exp'), may hold values from -2 to 2
- w_in: bfloat16 [64, 1024, 4096], P('exp', None, 'tok'), may hold values from -0.75 to 0.75
- w_out: bfloat16 [64, 4096, 1024], P('exp', 'tok'), may hold values from -0.1875 to 0.1875
Outputs:
- mixed: bfloat16 [12, 8192, 1024], P(None, 'tok', 'exp')
The draws below stay inside these ranges and needn't reach their ends.
All inputs are finite; a program needn't handle non-finite values.
Results may differ from the reference program's by a relative error of at most 0.0072.
Values may be sent and summed in bfloat16 or wider, within the bound.
A program may use at most 192 MiB of HBM per device.

```python
import math
import jax
import jax.numpy as jnp
from jax import lax

D = 1024
FF = 4096
EXPERTS = 64
SLOTS_PER = 2
SEQS = 12
SLOTS = 128
LEN = 8192


def slot_helper(key):
    raw = jax.random.normal(jax.random.fold_in(key, 11), (D, SLOTS), jnp.float32)
    return jnp.clip(raw, -6.0, 6.0) * (2.0 / math.sqrt(D))


def draw_slot_params(key, part):
    return slot_helper(key).astype(jnp.bfloat16)


def draw_tokens(key, part):
    base = jax.random.fold_in(key, 23)
    values = jnp.clip(jax.random.normal(base, (SEQS, LEN, D), jnp.float32), -6.0, 6.0)
    return values.astype(jnp.bfloat16)


def block_levels(key, dims, cuts, low, largest):
    def one(dim, blocks):
        draws = jax.random.uniform(jax.random.fold_in(jax.random.fold_in(key, 6), dim), (blocks,), jnp.float32, low / len(cuts), largest / len(cuts))
        return jnp.repeat(jnp.exp(draws), dims[dim] // blocks).reshape((-1,) + (1,) * (len(dims) - dim - 1))

    factor_of = one(*cuts[0])
    for cut in cuts[1:]:
        factor_of = factor_of * one(*cut)
    return factor_of


def bell_draw(key, extent, spread, most, pieces=(), dtype=jnp.bfloat16):
    drawn = jax.random.normal(key, extent, jnp.float32) * spread
    if len(pieces) > 0:
        drawn = block_levels(key, extent, pieces, -0.22, 0.18) * drawn
    return jnp.clip(drawn, min=-most, max=most).astype(dtype)


def setup_inputs(seed: int = 0) -> dict:
    arg_keys = jax.random.split(jax.random.key(seed), 5)
    return {
        "tokens": draw_tokens(jax.random.fold_in(arg_keys[4], 71), 0),
        "slot_params": draw_slot_params(jax.random.fold_in(arg_keys[4], 71), 0),
        "w_in": bell_draw(arg_keys[2], (EXPERTS, D, FF), (D // 16) ** -0.5, 0.75, ((0, 4), (2, 8))),
        "w_out": bell_draw(arg_keys[3], (EXPERTS, FF, D), (FF // 4) ** -0.5, 0.1875, ((0, 4), (1, 8))),
    }


def reference(tokens, slot_params, w_in, w_out):
    def per_sequence(seq_tokens):
        logits = jnp.dot(seq_tokens, slot_params, preferred_element_type=jnp.float32)
        dmax = jnp.max(logits, axis=0)
        dexp = jnp.exp(logits - dmax[None, :])
        den = jnp.sum(dexp, axis=0)
        dweight = dexp.astype(jnp.bfloat16)
        slot_sum = jnp.dot(dweight.T, seq_tokens, preferred_element_type=jnp.float32)
        slot_in = (slot_sum / den[:, None]).astype(jnp.bfloat16)
        cmax = jnp.max(logits, axis=1)
        cexp = jnp.exp(logits - cmax[:, None])
        cweight = (cexp / jnp.sum(cexp, axis=1)[:, None]).astype(jnp.bfloat16)
        return slot_in, cweight

    slot_in, cweight = lax.map(per_sequence, tokens)
    grouped = slot_in.reshape(SEQS, EXPERTS, SLOTS_PER, D).transpose(1, 0, 2, 3).reshape(EXPERTS, SEQS * SLOTS_PER, D)

    def per_expert(items):
        expert_in, first, second = items
        hidden = jax.nn.gelu(jnp.dot(expert_in, first, preferred_element_type=jnp.float32), approximate=True).astype(jnp.bfloat16)
        return jnp.dot(hidden, second, preferred_element_type=jnp.float32).astype(jnp.bfloat16)

    outputs = lax.map(per_expert, (grouped, w_in, w_out))
    slot_out = outputs.reshape(EXPERTS, SEQS, SLOTS_PER, D).transpose(1, 0, 2, 3).reshape(SEQS, SLOTS, D)

    def per_combine(items):
        weights, values = items
        return jnp.dot(weights, values, preferred_element_type=jnp.float32).astype(jnp.bfloat16)

    return lax.map(per_combine, (cweight, slot_out))
```

```python
import functools

import jax
import jax.numpy as jnp
from jax import lax
from jax.experimental import pallas as pl
from jax.experimental.pallas import tpu as pltpu
from jax.sharding import PartitionSpec as P

SLOTS_PER = 2
NZ, NY = 4, 2
NT = NZ * NY
NE = 4
LANES = 128
MESH = pl.DeviceIdType.MESH
F32, BF16 = jnp.float32, jnp.bfloat16


def gelu(v):
    return 0.5 * v * (1.0 + jnp.tanh(0.7978845608 * (v + 0.044715 * (v * v * v))))


def main_kernel(
    tok_hbm, prm_ref, win_hbm, wout_hbm, cw_hbm, g_hbm,
    tbuf, prm, win, wout, lg, cwbuf, part, psend, st, wrow, yrecv, zsend, zrecv, facc, xs,
    acc, bsend, byrecv, bzsend, bzrecv, fin, g,
    tsem, wsem, cwsem, gsem,
    p_s, p_r, s_s, s_r, y_s, y_r, z_s, z_r, az_s, az_r, ay_s, ay_r,
    by_s, by_r, bz_s, bz_r, c_s, c_r, gz_s, gz_r, gy_s, gy_r,
):
    seqs, _, width = tok_hbm.shape
    own_w = prm_ref.shape[0]
    pair_rows = acc.shape[0]
    half_rows = pair_rows // 2
    feat = g.shape[3]
    t = lax.axis_index("tok")
    e = lax.axis_index("exp")
    z, y = t // NY, t % NY
    oy = 1 - y
    me = y * NZ + z

    def remote(src, dst, ssem, rsem, tok, exp):
        return pltpu.make_async_remote_copy(
            src_ref=src, dst_ref=dst, send_sem=ssem, recv_sem=rsem,
            device_id={"tok": tok, "exp": exp}, device_id_type=MESH)

    def zpeer(d):
        return lax.rem(z + d, NZ)

    def tok_copy(s):
        slot = lax.rem(s, 3)
        return pltpu.make_async_copy(tok_hbm.at[s], tbuf.at[slot], tsem.at[slot])

    def w_copies(p):
        return (pltpu.make_async_copy(win_hbm.at[pl.ds(2 * p, 2)], win.at[pl.ds(2 * p, 2)], wsem.at[0, p]),
                pltpu.make_async_copy(wout_hbm.at[pl.ds(2 * p, 2)], wout.at[pl.ds(2 * p, 2)], wsem.at[1, p]))

    def cw_copy(s):
        return pltpu.make_async_copy(cwbuf.at[s], cw_hbm.at[s], cwsem.at[s])

    tok_copy(0).start()
    tok_copy(1).start()

    barrier = pltpu.get_barrier_semaphore()
    for d in range(1, NT):
        pl.semaphore_signal(barrier, inc=1, device_id={"tok": lax.rem(t + d, NT), "exp": e}, device_id_type=MESH)
    for d in range(1, NE):
        pl.semaphore_signal(barrier, inc=1, device_id={"tok": t, "exp": lax.rem(e + d, NE)}, device_id_type=MESH)
    pl.semaphore_wait(barrier, NT + NE - 2)

    own_cols = pl.ds(pl.multiple_of(e * own_w, own_w), own_w)
    p_copies = [remote(prm_ref, prm.at[own_cols], p_s.at[d - 1], p_r.at[d - 1], t, lax.rem(e + d, NE)) for d in range(1, NE)]
    for c in p_copies:
        c.start()
    prm[own_cols, :] = prm_ref[...]
    st[me] = jnp.ones((own_w, LANES), F32)
    for c in p_copies:
        c.wait()

    lane = lax.broadcasted_iota(jnp.int32, (own_w, LANES), 1)

    def dispatch(s, carry):
        @pl.when(s + 2 < seqs)
        def _():
            tok_copy(s + 2).start()

        @pl.when(s < NT)
        def _():
            for c in w_copies(s):
                c.start()

        tok_copy(s).wait()
        slot = lax.rem(s, 3)
        logits = lax.dot_general(prm[...], tbuf[slot], (((1,), (1,)), ((), ())), preferred_element_type=F32)
        lg[...] = logits
        ex = jnp.exp(logits - jnp.max(logits, axis=0, keepdims=True))
        cwbuf[s] = (ex / jnp.sum(ex, axis=0, keepdims=True)).astype(BF16)
        cw_copy(s).start()
        own = lg[own_cols, :]
        peak = jnp.max(own, axis=1, keepdims=True)
        dx = jnp.exp(own - peak)
        den = jnp.sum(dx, axis=1, keepdims=True)
        ssum = jnp.dot(dx.astype(BF16), tbuf[slot], preferred_element_type=F32)
        scaled = ssum / den
        for k in range(NT):
            part[k, pl.ds(s, own_w, stride=seqs), :] = scaled[:, k * LANES:(k + 1) * LANES]
        st[me] = jnp.where(lane == s, peak, jnp.where(lane == s + 64, den, st[me]))
        return carry

    lax.fori_loop(0, seqs, dispatch, 0)

    s_copies = [remote(st.at[me], st.at[me], s_s.at[d - 1], s_r.at[d - 1], lax.rem(t + d, NT), e) for d in range(1, NT)]
    for c in s_copies:
        c.start()
    y_tok = z * NY + oy
    y_copies = {}
    for d in (1, 2, 3, 0):
        zz = zpeer(d)
        psend[zz] = part[oy * NZ + zz].astype(BF16)
        y_copies[d] = remote(psend.at[zz], yrecv.at[zz], y_s.at[d], y_r.at[d], y_tok, e)
        y_copies[d].start()
    for c in s_copies:
        c.wait()
    peaks = [st[r] for r in range(NT)]
    top = functools.reduce(jnp.maximum, peaks)
    total = jnp.zeros_like(top)
    for r in range(NT):
        total += pltpu.roll(peaks[r], 64, 1) * jnp.exp(peaks[r] - top)
    for i, r in enumerate((me, oy * NZ + z)):
        mine = st[r]
        w = pltpu.roll(mine, 64, 1) * jnp.exp(mine - top) / total
        for s in range(seqs):
            wrow[i, pl.ds(s, own_w, stride=seqs), :] = jnp.broadcast_to(w[:, s:s + 1], (own_w, LANES))

    z_copies = []
    for d in (1, 2, 3, 0):
        zz = zpeer(d)
        y_copies[d].wait()
        both = part[y * NZ + zz] * wrow[0] + yrecv[zz].astype(F32) * wrow[1]
        if d:
            zsend[zz] = both.astype(BF16)
            c = remote(zsend.at[zz], zrecv.at[d - 1], z_s.at[d - 1], z_r.at[d - 1], zz * NY + y, e)
            c.start()
            z_copies.append(c)
        else:
            facc[...] = both
    for c in z_copies:
        c.wait()
    xs[me] = (facc[...] + zrecv[0].astype(F32) + zrecv[1].astype(F32) + zrecv[2].astype(F32)).astype(BF16)

    def gather(block, zs, zr, ys, yr):
        zc = [remote(block(me), block(me), zs.at[d - 1], zr.at[d - 1], zpeer(d) * NY + y, e) for d in range(1, NZ)]
        yc = [remote(block(me), block(me), ys.at[0], yr.at[0], y_tok, e)]
        for c in zc:
            c.start()
        yc[0].start()
        for d in range(1, NZ):
            zc[d - 1].wait_recv()
            got = y * NZ + lax.rem(z + NZ - d, NZ)
            c = remote(block(got), block(got), ys.at[d], yr.at[d], y_tok, e)
            c.start()
            yc.append(c)
        for c in zc:
            c.wait_send()
        for c in yc:
            c.wait()

    gather(lambda r: xs.at[r], az_s, az_r, ay_s, ay_r)

    upper = lax.broadcasted_iota(jnp.int32, (pair_rows, 1), 0) < half_rows

    def by_copy(d):
        zz = zpeer(d)
        return remote(bsend.at[zz], byrecv.at[zz], by_s.at[d], by_r.at[d], y_tok, e)

    def bz_copy(d):
        zz = zpeer(d)
        return remote(bzsend.at[zz], bzrecv.at[d - 1], bz_s.at[d - 1], bz_r.at[d - 1], zz * NY + y, e)

    def expert_pair(i, carry):
        d = lax.rem(i + 1, NZ)
        zz = zpeer(d)
        first = i < NZ
        p = jnp.where(first, oy, y) * NZ + zz
        for c in w_copies(p):
            c.wait()
        rows = pl.ds(pl.multiple_of(p * pair_rows, 16), pair_rows)
        x = jnp.concatenate([xs[k, rows, :] for k in range(NT)], axis=1)
        h0 = jnp.dot(x, win[2 * p], preferred_element_type=F32)
        h1 = jnp.dot(x, win[2 * p + 1], preferred_element_type=F32)
        hid = gelu(jnp.where(upper, h0, h1))
        zero = jnp.zeros_like(hid)
        u0 = jnp.where(upper, hid, zero).astype(BF16)
        u1 = jnp.where(upper, zero, hid).astype(BF16)
        acc[...] = (jnp.dot(u0, wout[2 * p], preferred_element_type=F32)
                    + jnp.dot(u1, wout[2 * p + 1], preferred_element_type=F32))

        @pl.when(first)
        def _():
            bsend[zz] = acc[...].astype(BF16)
            by_copy(d).start()

        @pl.when(jnp.logical_not(first))
        def _():
            by_copy(d).wait()
            acc[...] += byrecv[zz].astype(F32)

            @pl.when(i < 2 * NZ - 1)
            def _():
                bzsend[zz] = acc[...].astype(BF16)
                bz_copy(d).start()

        return carry

    lax.fori_loop(0, NT, expert_pair, 0)

    for d in range(1, NZ):
        bz_copy(d).wait()
    done = (acc[...] + bzrecv[0].astype(F32) + bzrecv[1].astype(F32) + bzrecv[2].astype(F32)).astype(BF16)
    for k in range(NE):
        fin[k] = done[:, k * feat:(k + 1) * feat]
    c_copies = []
    for d in range(1, NE):
        to = lax.rem(e + d, NE)
        c = remote(fin.at[to], g.at[e, me], c_s.at[d - 1], c_r.at[d - 1], t, to)
        c.start()
        c_copies.append(c)
    g[e, me] = fin[e]
    for c in c_copies:
        c.wait()
    gather(lambda r: g.at[:, r], gz_s, gz_r, gy_s, gy_r)
    out = pltpu.make_async_copy(g, g_hbm, gsem)
    out.start()
    for s in range(seqs):
        cw_copy(s).wait()
    out.wait()


def combine_kernel(cw_ref, g_ref, o_ref, wide):
    s = pl.program_id(0)
    slots = cw_ref.shape[1]
    tiles, rows, _ = wide.shape
    seqs = rows // slots

    @pl.when(s == 0)
    def _():
        for c in range(tiles):
            wide[c] = g_ref[:, c * LANES:(c + 1) * LANES].astype(F32)

    vals = jnp.concatenate([wide[c, pl.ds(s, slots, stride=seqs), :] for c in range(tiles)], axis=1).astype(BF16)
    o_ref[0] = lax.dot_general(cw_ref[0], vals, (((0,), (0,)), ((), ())), preferred_element_type=F32).astype(BF16)


def fused(tokens, slot_params, w_in, w_out):
    seqs, length, width = tokens.shape
    own_w = slot_params.shape[1]
    slots = own_w * NE
    experts, _, ff = w_in.shape
    rows = seqs * own_w
    pair_rows = rows // NT
    feat = width // NE
    dma = pltpu.SemaphoreType.DMA
    any_spec = pl.BlockSpec(memory_space=pl.ANY)
    cw, g = pl.pallas_call(
        main_kernel,
        out_shape=(jax.ShapeDtypeStruct((seqs, slots, length), BF16),
                   jax.ShapeDtypeStruct((NE, NT, pair_rows, feat), BF16)),
        in_specs=[any_spec, pl.BlockSpec(memory_space=pltpu.VMEM), any_spec, any_spec],
        out_specs=(any_spec, any_spec),
        scratch_shapes=[
            pltpu.VMEM((3, length, width), BF16),
            pltpu.VMEM((slots, width), BF16),
            pltpu.VMEM((experts, width, ff), BF16),
            pltpu.VMEM((experts, ff, width), BF16),
            pltpu.VMEM((slots, length), F32),
            pltpu.VMEM((seqs, slots, length), BF16),
            pltpu.VMEM((NT, rows, LANES), F32),
            pltpu.VMEM((NZ, rows, LANES), BF16),
            pltpu.VMEM((NT, own_w, LANES), F32),
            pltpu.VMEM((2, rows, LANES), F32),
            pltpu.VMEM((NZ, rows, LANES), BF16),
            pltpu.VMEM((NZ, rows, LANES), BF16),
            pltpu.VMEM((NZ - 1, rows, LANES), BF16),
            pltpu.VMEM((rows, LANES), F32),
            pltpu.VMEM((NT, rows, LANES), BF16),
            pltpu.VMEM((pair_rows, width), F32),
            pltpu.VMEM((NZ, pair_rows, width), BF16),
            pltpu.VMEM((NZ, pair_rows, width), BF16),
            pltpu.VMEM((NZ, pair_rows, width), BF16),
            pltpu.VMEM((NZ - 1, pair_rows, width), BF16),
            pltpu.VMEM((NE, pair_rows, feat), BF16),
            pltpu.VMEM((NE, NT, pair_rows, feat), BF16),
            dma((3,)), dma((2, NT)), dma((seqs,)), dma,
            dma((NE - 1,)), dma((NE - 1,)),
            dma((NT - 1,)), dma((NT - 1,)),
            dma((NZ,)), dma((NZ,)),
            dma((NZ - 1,)), dma((NZ - 1,)),
            dma((NZ - 1,)), dma((NZ - 1,)),
            dma((NZ,)), dma((NZ,)),
            dma((NZ,)), dma((NZ,)),
            dma((NZ - 1,)), dma((NZ - 1,)),
            dma((NE - 1,)), dma((NE - 1,)),
            dma((NZ - 1,)), dma((NZ - 1,)),
            dma((NZ,)), dma((NZ,)),
        ],
        compiler_params=pltpu.CompilerParams(collective_id=0, has_side_effects=True, vmem_limit_bytes=60 << 20),
        name="dispatch_experts",
    )(tokens, slot_params.T, w_in, w_out)
    return pl.pallas_call(
        combine_kernel,
        grid=(seqs,),
        out_shape=jax.ShapeDtypeStruct((seqs, length, feat), BF16),
        in_specs=[pl.BlockSpec((1, slots, length), lambda s: (s, 0, 0)),
                  pl.BlockSpec((slots * seqs, feat), lambda s: (0, 0))],
        out_specs=pl.BlockSpec((1, length, feat), lambda s: (s, 0, 0)),
        scratch_shapes=[pltpu.VMEM((feat // LANES, slots * seqs, LANES), F32)],
        compiler_params=pltpu.CompilerParams(vmem_limit_bytes=32 << 20),
        name="combine",
    )(cw, g.reshape(slots * seqs, feat))


def shards(tokens, slot_params, w_in, w_out):
    own_width = slot_params.shape[1]
    own_logits = jnp.einsum("std,dj->sjt", tokens, slot_params, preferred_element_type=jnp.float32)
    all_logits = lax.all_gather(own_logits, "exp", axis=1, tiled=True)
    local_max = jnp.max(own_logits, axis=2)
    slot_peak = lax.pmax(local_max, "tok")
    dexp = jnp.exp(own_logits - slot_peak[:, :, None])
    local_den = jnp.sum(dexp, axis=2)
    dweight = dexp.astype(jnp.bfloat16)
    local_sum = jnp.einsum("sjt,std->sjd", dweight, tokens, preferred_element_type=jnp.float32)
    slot_sum, slot_den = lax.psum((local_sum, local_den), "tok")
    slot_in = (slot_sum / slot_den[:, :, None]).astype(jnp.bfloat16)
    seq_count = tokens.shape[0]
    local_experts = w_in.shape[0]
    width = tokens.shape[2]
    grouped = slot_in.reshape(seq_count, local_experts, SLOTS_PER, width)
    hidden = jax.nn.gelu(
        jnp.einsum("sepd,edf->sepf", grouped, w_in, preferred_element_type=jnp.float32),
        approximate=True,
    ).astype(jnp.bfloat16)
    partial_out = jnp.einsum("sepf,efd->sepd", hidden, w_out, preferred_element_type=jnp.float32)
    partial_out = partial_out.reshape(seq_count, own_width, width)
    summed = lax.psum(partial_out, "tok").astype(jnp.bfloat16)
    slot_out = lax.all_to_all(summed, "exp", split_axis=2, concat_axis=1, tiled=True)
    comb_max = jnp.max(all_logits, axis=1)
    cexp = jnp.exp(all_logits - comb_max[:, None, :])
    cweight = (cexp / jnp.sum(cexp, axis=1)[:, None, :]).astype(jnp.bfloat16)
    mixed = jnp.einsum("sjt,sjd->std", cweight, slot_out, preferred_element_type=jnp.float32)
    return mixed.astype(jnp.bfloat16)


def solution(mesh):
    quick = mesh.shape["tok"] == NT and mesh.shape["exp"] == NE
    return jax.shard_map(
        fused if quick else shards,
        mesh=mesh,
        in_specs=(
            P(None, "tok", None),
            P(None, "exp"),
            P("exp", None, "tok"),
            P("exp", "tok", None),
        ),
        out_specs=P(None, "tok", "exp"),
        check_vma=False,
    )
```

```python
import functools

import jax
import jax.numpy as jnp
from jax import lax
from jax.experimental import pallas as pl
from jax.experimental.pallas import tpu as pltpu
from jax.sharding import PartitionSpec as P

SLOTS_PER = 2
NZ, NY = 4, 2
NT = NZ * NY
NE = 4
NG = 3
LANES = 128
MESH = pl.DeviceIdType.MESH
F32, BF16 = jnp.float32, jnp.bfloat16


def gelu(v):
    return 0.5 * v * (1.0 + jnp.tanh(0.7978845608 * (v + 0.044715 * (v * v * v))))


def main_kernel(
    tok_hbm, prm_ref, win_hbm, wout_hbm, cw_hbm, g_hbm,
    tbuf, prm, win, wout, lg, cwbuf, part, psend, st, wrow, yrecv, zsend, zrecv, facc, xs,
    acc, bsend, byrecv, bzsend, bzrecv, fin, g,
    tsem, wsem, cwsem, gsem,
    p_s, p_r, s_s, s_r, y_s, y_r, z_s, z_r, az_s, az_r, ay_s, ay_r,
    by_s, by_r, bz_s, bz_r, c_s, c_r, gl_s, gl_r, gr_s, gr_r, gy_s, gy_r,
):
    seqs, _, width = tok_hbm.shape
    own_w = prm_ref.shape[0]
    pair_rows = acc.shape[0]
    group = seqs // NG
    own_rows = own_w * group
    pair_part = pair_rows // NG
    feat = g.shape[3]
    t = lax.axis_index("tok")
    e = lax.axis_index("exp")
    z, y = t // NY, t % NY
    oy = 1 - y
    me = y * NZ + z

    def remote(src, dst, ssem, rsem, tok, exp):
        return pltpu.make_async_remote_copy(
            src_ref=src, dst_ref=dst, send_sem=ssem, recv_sem=rsem,
            device_id={"tok": tok, "exp": exp}, device_id_type=MESH)

    def zpeer(d):
        return lax.rem(z + d, NZ)

    def tok_copy(s):
        slot = lax.rem(s, 3)
        return pltpu.make_async_copy(tok_hbm.at[s], tbuf.at[slot], tsem.at[slot])

    def w_copies(p):
        return (pltpu.make_async_copy(win_hbm.at[pl.ds(2 * p, 2)], win.at[pl.ds(2 * p, 2)], wsem.at[0, p]),
                pltpu.make_async_copy(wout_hbm.at[pl.ds(2 * p, 2)], wout.at[pl.ds(2 * p, 2)], wsem.at[1, p]))

    def cw_copy(s):
        return pltpu.make_async_copy(cwbuf.at[s], cw_hbm.at[s], cwsem.at[s])

    tok_copy(0).start()
    tok_copy(1).start()

    barrier = pltpu.get_barrier_semaphore()
    for d in range(1, NT):
        pl.semaphore_signal(barrier, inc=1, device_id={"tok": lax.rem(t + d, NT), "exp": e}, device_id_type=MESH)
    for d in range(1, NE):
        pl.semaphore_signal(barrier, inc=1, device_id={"tok": t, "exp": lax.rem(e + d, NE)}, device_id_type=MESH)
    pl.semaphore_wait(barrier, NT + NE - 2)

    own_cols = pl.ds(pl.multiple_of(e * own_w, own_w), own_w)
    p_copies = [remote(prm_ref, prm.at[own_cols], p_s.at[d - 1], p_r.at[d - 1], t, lax.rem(e + d, NE)) for d in range(1, NE)]
    for c in p_copies:
        c.start()
    prm[own_cols, :] = prm_ref[...]
    for i in range(NG):
        st[i, me] = jnp.ones((own_w, LANES), F32)
    for c in p_copies:
        c.wait()

    lane = lax.broadcasted_iota(jnp.int32, (own_w, LANES), 1)

    def dispatch(s, carry):
        @pl.when(s + 2 < seqs)
        def _():
            tok_copy(s + 2).start()

        @pl.when(s >= seqs - NT)
        def _():
            for c in w_copies(s - (seqs - NT)):
                c.start()

        tok_copy(s).wait()
        slot = lax.rem(s, 3)
        gi, in_group = s // group, lax.rem(s, group)
        logits = lax.dot_general(prm[...], tbuf[slot], (((1,), (1,)), ((), ())), preferred_element_type=F32)
        lg[...] = logits
        ex = jnp.exp(logits - jnp.max(logits, axis=0, keepdims=True))
        cwbuf[s] = (ex / jnp.sum(ex, axis=0, keepdims=True)).astype(BF16)
        cw_copy(s).start()
        own = lg[own_cols, :]
        peak = jnp.max(own, axis=1, keepdims=True)
        dx = jnp.exp(own - peak)
        den = jnp.sum(dx, axis=1, keepdims=True)
        ssum = jnp.dot(dx.astype(BF16), tbuf[slot], preferred_element_type=F32)
        scaled = ssum / den
        for k in range(NT):
            part[k, gi, pl.ds(in_group, own_w, stride=group), :] = scaled[:, k * LANES:(k + 1) * LANES]
        st[gi, me] = jnp.where(lane == in_group, peak, jnp.where(lane == in_group + 64, den, st[gi, me]))
        return carry

    y_tok = z * NY + oy
    flight = {}

    def send_partial(i):
        stats = [remote(st.at[i, me], st.at[i, me], s_s.at[i, d - 1], s_r.at[i, d - 1], lax.rem(t + d, NT), e) for d in range(1, NT)]
        for c in stats:
            c.start()
        for zz in range(NZ):
            psend[i, zz] = part[oy * NZ + zz, i].astype(BF16)
        c = remote(psend.at[i], yrecv.at[i], y_s.at[i], y_r.at[i], y_tok, e)
        c.start()
        flight[i] = stats + [c]

    def reduce_y(i):
        for c in flight[i]:
            c.wait()
        peaks = [st[i, r] for r in range(NT)]
        top = functools.reduce(jnp.maximum, peaks)
        total = jnp.zeros_like(top)
        for r in range(NT):
            total += pltpu.roll(peaks[r], 64, 1) * jnp.exp(peaks[r] - top)
        for n, r in enumerate((me, oy * NZ + z)):
            mine = st[i, r]
            w = pltpu.roll(mine, 64, 1) * jnp.exp(mine - top) / total
            for q in range(group):
                wrow[n, pl.ds(q, own_w, stride=group), :] = jnp.broadcast_to(w[:, q:q + 1], (own_w, LANES))
        copies = []
        for d in (1, 2, 3, 0):
            zz = zpeer(d)
            both = part[y * NZ + zz, i] * wrow[0] + yrecv[i, zz].astype(F32) * wrow[1]
            if d:
                zsend[i, zz] = both.astype(BF16)
                c = remote(zsend.at[i, zz], zrecv.at[i, d - 1], z_s.at[i, d - 1], z_r.at[i, d - 1], zz * NY + y, e)
                c.start()
                copies.append(c)
            else:
                facc[i] = both
        flight[i] = copies

    def finish_z(i):
        for c in flight[i]:
            c.wait()
        xs[i, me] = (facc[i] + zrecv[i, 0].astype(F32) + zrecv[i, 1].astype(F32) + zrecv[i, 2].astype(F32)).astype(BF16)
        zc = [remote(xs.at[i, me], xs.at[i, me], az_s.at[i, d - 1], az_r.at[i, d - 1], zpeer(d) * NY + y, e) for d in range(1, NZ)]
        yc = remote(xs.at[i, me], xs.at[i, me], ay_s.at[i, 0], ay_r.at[i, 0], y_tok, e)
        for c in zc:
            c.start()
        yc.start()
        flight[i] = (zc, [yc])

    def forward(i):
        zc, yc = flight[i]
        for d in range(1, NZ):
            zc[d - 1].wait_recv()
            got = y * NZ + lax.rem(z + NZ - d, NZ)
            c = remote(xs.at[i, got], xs.at[i, got], ay_s.at[i, d], ay_r.at[i, d], y_tok, e)
            c.start()
            yc.append(c)

    def settle(i):
        zc, yc = flight[i]
        for c in zc:
            c.wait_send()
        for c in yc:
            c.wait()

    half = group // 2

    def run(i):
        lax.fori_loop(i * half, (i + 1) * half, dispatch, 0)

    run(0)
    run(1)
    send_partial(0)
    run(2)
    reduce_y(0)
    run(3)
    finish_z(0)
    send_partial(1)
    run(4)
    reduce_y(1)
    forward(0)
    run(5)
    send_partial(2)
    finish_z(1)
    reduce_y(2)
    forward(1)
    finish_z(2)
    settle(0)
    forward(2)
    settle(1)
    settle(2)

    upper = lax.rem(lax.broadcasted_iota(jnp.int32, (pair_rows, 1), 0), pair_part) < pair_part // 2

    def by_copy(d):
        zz = zpeer(d)
        return remote(bsend.at[zz], byrecv.at[zz], by_s.at[d], by_r.at[d], y_tok, e)

    def bz_copy(d):
        zz = zpeer(d)
        return remote(bzsend.at[zz], bzrecv.at[d - 1], bz_s.at[d - 1], bz_r.at[d - 1], zz * NY + y, e)

    def expert_pair(i, carry):
        d = lax.rem(i + 1, NZ)
        zz = zpeer(d)
        first = i < NZ
        p = jnp.where(first, oy, y) * NZ + zz
        for c in w_copies(p):
            c.wait()
        rows = pl.ds(pl.multiple_of(p * pair_part, 16), pair_part)
        x = jnp.concatenate([jnp.concatenate([xs[i, k, rows, :] for k in range(NT)], axis=1) for i in range(NG)], axis=0)
        h0 = jnp.dot(x, win[2 * p], preferred_element_type=F32)
        h1 = jnp.dot(x, win[2 * p + 1], preferred_element_type=F32)
        hid = gelu(jnp.where(upper, h0, h1))
        zero = jnp.zeros_like(hid)
        u0 = jnp.where(upper, hid, zero).astype(BF16)
        u1 = jnp.where(upper, zero, hid).astype(BF16)
        acc[...] = (jnp.dot(u0, wout[2 * p], preferred_element_type=F32)
                    + jnp.dot(u1, wout[2 * p + 1], preferred_element_type=F32))

        @pl.when(first)
        def _():
            bsend[zz] = acc[...].astype(BF16)
            by_copy(d).start()

        @pl.when(jnp.logical_not(first))
        def _():
            by_copy(d).wait()
            acc[...] += byrecv[zz].astype(F32)

            @pl.when(i < 2 * NZ - 1)
            def _():
                bzsend[zz] = acc[...].astype(BF16)
                bz_copy(d).start()

        return carry

    lax.fori_loop(0, NT, expert_pair, 0)

    for d in range(1, NZ):
        bz_copy(d).wait()
    done = (acc[...] + bzrecv[0].astype(F32) + bzrecv[1].astype(F32) + bzrecv[2].astype(F32)).astype(BF16)
    for k in range(NE):
        fin[k] = done[:, k * feat:(k + 1) * feat]
    c_copies = []
    for d in range(1, NE):
        to = lax.rem(e + d, NE)
        c = remote(fin.at[to], g.at[e, me], c_s.at[d - 1], c_r.at[d - 1], t, to)
        c.start()
        c_copies.append(c)
    g[e, me] = fin[e]
    for c in c_copies:
        c.wait()

    def block(zz):
        return g.at[:, y * NZ + zz]

    def hop(zz, sems, n, step):
        to = jnp.clip(z + step, 0, NZ - 1) * NY + y
        return remote(block(zz), block(zz), sems[0].at[n], sems[1].at[n], to, e)

    def cross(zz, n):
        return remote(block(zz), block(zz), gy_s.at[n], gy_r.at[n], y_tok, e)

    ways = ((1, (gr_s, gr_r), 0), (-1, (gl_s, gl_r), NZ - 1))
    for step, sems, off in ways:
        @pl.when(z != NZ - 1 if step == 1 else z != 0)
        def _():
            hop(z, sems, 0, step).start()
    cross(z, 0).start()
    for n in range(1, NZ):
        for step, sems, off in ways:
            zz = z - step * n
            inside = zz >= 0 if step == 1 else zz < NZ
            at = jnp.clip(zz, 0, NZ - 1)
            more = jnp.logical_and(inside, z != NZ - 1 if step == 1 else z != 0)

            @pl.when(inside)
            def _():
                hop(at, sems, n - 1, -step).wait_recv()
                cross(at, off + n).start()

            if n < NZ - 1:
                @pl.when(more)
                def _():
                    hop(at, sems, n, step).start()
    for step, sems, off in ways:
        @pl.when(z != NZ - 1 if step == 1 else z != 0)
        def _():
            hop(z, sems, 0, step).wait_send()
    cross(z, 0).wait()
    for n in range(1, NZ):
        for step, sems, off in ways:
            zz = z - step * n
            inside = zz >= 0 if step == 1 else zz < NZ
            at = jnp.clip(zz, 0, NZ - 1)
            more = jnp.logical_and(inside, z != NZ - 1 if step == 1 else z != 0)

            @pl.when(inside)
            def _():
                cross(at, off + n).wait()

            if n < NZ - 1:
                @pl.when(more)
                def _():
                    hop(at, sems, n, step).wait_send()
    out = pltpu.make_async_copy(g, g_hbm, gsem)
    out.start()
    for s in range(seqs):
        cw_copy(s).wait()
    out.wait()


def combine_kernel(cw_ref, g_ref, o_ref, wide):
    seqs_here, slots, _ = cw_ref.shape
    tiles, groups, _, _ = wide.shape
    blocks = g_ref.shape[0]
    span = g_ref.shape[1] // groups
    size = pl.num_programs(0) * seqs_here // groups

    @pl.when(pl.program_id(0) == 0)
    def _():
        for c in range(tiles):
            for i in range(groups):
                part = g_ref[:, i * span:(i + 1) * span, c * LANES:(c + 1) * LANES]
                wide[c, i] = part.astype(F32).reshape(blocks * span, LANES)

    for n in range(seqs_here):
        s = pl.program_id(0) * seqs_here + n
        i, q = s // size, lax.rem(s, size)
        vals = jnp.concatenate([wide[c, i, pl.ds(q, slots, stride=size), :] for c in range(tiles)], axis=1).astype(BF16)
        o_ref[n] = lax.dot_general(cw_ref[n], vals, (((0,), (0,)), ((), ())), preferred_element_type=F32).astype(BF16)


def fused(tokens, slot_params, w_in, w_out):
    seqs, length, width = tokens.shape
    own_w = slot_params.shape[1]
    slots = own_w * NE
    experts, _, ff = w_in.shape
    rows = seqs * own_w
    pair_rows = rows // NT
    own_rows = rows // NG
    step = 2
    feat = width // NE
    dma = pltpu.SemaphoreType.DMA
    any_spec = pl.BlockSpec(memory_space=pl.ANY)
    cw, g = pl.pallas_call(
        main_kernel,
        out_shape=(jax.ShapeDtypeStruct((seqs, slots, length), BF16),
                   jax.ShapeDtypeStruct((NE, NT, pair_rows, feat), BF16)),
        in_specs=[any_spec, pl.BlockSpec(memory_space=pltpu.VMEM), any_spec, any_spec],
        out_specs=(any_spec, any_spec),
        scratch_shapes=[
            pltpu.VMEM((3, length, width), BF16),
            pltpu.VMEM((slots, width), BF16),
            pltpu.VMEM((experts, width, ff), BF16),
            pltpu.VMEM((experts, ff, width), BF16),
            pltpu.VMEM((slots, length), F32),
            pltpu.VMEM((seqs, slots, length), BF16),
            pltpu.VMEM((NT, NG, own_rows, LANES), F32),
            pltpu.VMEM((NG, NZ, own_rows, LANES), BF16),
            pltpu.VMEM((NG, NT, own_w, LANES), F32),
            pltpu.VMEM((2, own_rows, LANES), F32),
            pltpu.VMEM((NG, NZ, own_rows, LANES), BF16),
            pltpu.VMEM((NG, NZ, own_rows, LANES), BF16),
            pltpu.VMEM((NG, NZ - 1, own_rows, LANES), BF16),
            pltpu.VMEM((NG, own_rows, LANES), F32),
            pltpu.VMEM((NG, NT, own_rows, LANES), BF16),
            pltpu.VMEM((pair_rows, width), F32),
            pltpu.VMEM((NZ, pair_rows, width), BF16),
            pltpu.VMEM((NZ, pair_rows, width), BF16),
            pltpu.VMEM((NZ, pair_rows, width), BF16),
            pltpu.VMEM((NZ - 1, pair_rows, width), BF16),
            pltpu.VMEM((NE, pair_rows, feat), BF16),
            pltpu.VMEM((NE, NT, pair_rows, feat), BF16),
            dma((3,)), dma((2, NT)), dma((seqs,)), dma,
            dma((NE - 1,)), dma((NE - 1,)),
            dma((NG, NT - 1)), dma((NG, NT - 1)),
            dma((NG,)), dma((NG,)),
            dma((NG, NZ - 1)), dma((NG, NZ - 1)),
            dma((NG, NZ - 1)), dma((NG, NZ - 1)),
            dma((NG, NZ)), dma((NG, NZ)),
            dma((NZ,)), dma((NZ,)),
            dma((NZ - 1,)), dma((NZ - 1,)),
            dma((NE - 1,)), dma((NE - 1,)),
            dma((NZ - 1,)), dma((NZ - 1,)),
            dma((NZ - 1,)), dma((NZ - 1,)),
            dma((2 * NZ - 1,)), dma((2 * NZ - 1,)),
        ],
        compiler_params=pltpu.CompilerParams(collective_id=0, has_side_effects=True, vmem_limit_bytes=60 << 20),
        name="dispatch_experts",
    )(tokens, slot_params.T, w_in, w_out)
    return pl.pallas_call(
        combine_kernel,
        grid=(seqs // step,),
        out_shape=jax.ShapeDtypeStruct((seqs, length, feat), BF16),
        in_specs=[pl.BlockSpec((step, slots, length), lambda s: (s, 0, 0)),
                  pl.BlockSpec((NE * NT, pair_rows, feat), lambda s: (0, 0, 0))],
        out_specs=pl.BlockSpec((step, length, feat), lambda s: (s, 0, 0)),
        scratch_shapes=[pltpu.VMEM((feat // LANES, NG, slots * seqs // NG, LANES), F32)],
        compiler_params=pltpu.CompilerParams(vmem_limit_bytes=60 << 20),
        name="combine",
    )(cw, g.reshape(NE * NT, pair_rows, feat))


def shards(tokens, slot_params, w_in, w_out):
    own_width = slot_params.shape[1]
    own_logits = jnp.einsum("std,dj->sjt", tokens, slot_params, preferred_element_type=jnp.float32)
    all_logits = lax.all_gather(own_logits, "exp", axis=1, tiled=True)
    local_max = jnp.max(own_logits, axis=2)
    slot_peak = lax.pmax(local_max, "tok")
    dexp = jnp.exp(own_logits - slot_peak[:, :, None])
    local_den = jnp.sum(dexp, axis=2)
    dweight = dexp.astype(jnp.bfloat16)
    local_sum = jnp.einsum("sjt,std->sjd", dweight, tokens, preferred_element_type=jnp.float32)
    slot_sum, slot_den = lax.psum((local_sum, local_den), "tok")
    slot_in = (slot_sum / slot_den[:, :, None]).astype(jnp.bfloat16)
    seq_count = tokens.shape[0]
    local_experts = w_in.shape[0]
    width = tokens.shape[2]
    grouped = slot_in.reshape(seq_count, local_experts, SLOTS_PER, width)
    hidden = jax.nn.gelu(
        jnp.einsum("sepd,edf->sepf", grouped, w_in, preferred_element_type=jnp.float32),
        approximate=True,
    ).astype(jnp.bfloat16)
    partial_out = jnp.einsum("sepf,efd->sepd", hidden, w_out, preferred_element_type=jnp.float32)
    partial_out = partial_out.reshape(seq_count, own_width, width)
    summed = lax.psum(partial_out, "tok").astype(jnp.bfloat16)
    slot_out = lax.all_to_all(summed, "exp", split_axis=2, concat_axis=1, tiled=True)
    comb_max = jnp.max(all_logits, axis=1)
    cexp = jnp.exp(all_logits - comb_max[:, None, :])
    cweight = (cexp / jnp.sum(cexp, axis=1)[:, None, :]).astype(jnp.bfloat16)
    mixed = jnp.einsum("sjt,sjd->std", cweight, slot_out, preferred_element_type=jnp.float32)
    return mixed.astype(jnp.bfloat16)


def solution(mesh):
    quick = mesh.shape["tok"] == NT and mesh.shape["exp"] == NE
    return jax.shard_map(
        fused if quick else shards,
        mesh=mesh,
        in_specs=(
            P(None, "tok", None),
            P(None, "exp"),
            P("exp", None, "tok"),
            P("exp", "tok", None),
        ),
        out_specs=P(None, "tok", "exp"),
        check_vma=False,
    )
```
